32 devices in a mesh: lat: 8 (over y, x, core), lon: 4 (over z).
Axes of the slice: x: 2, y: 2, z: 4, core: 2. Of those that a mesh axis runs over, the one named last changes fastest.
Arguments:
- ocean_state: bfloat16 [72, 1024, 128], P('lat', 'lon'), may hold values from -6 to 6
- cotangent: bfloat16 [72, 1024, 128], P('lat', 'lon'), may hold values from -6 to 6
- atm_embed: bfloat16 [16384, 256], P(('lat', 'lon')), may hold values from -6 to 6
- projection: bfloat16 [256, 128], replicated, may hold values from -0.375 to 0.375
- dw_kernel: float32 [7, 7, 128], replicated, may hold values from -0.875 to 0.875
- norm_gain: float32 [128], replicated, may hold values from 0.25 to 1.75
- w_in: bfloat16 [128, 512], replicated, may hold values from -0.5 to 0.5
- w_out: bfloat16 [512, 128], replicated, may hold values from -0.25 to 0.25
- margin_index: int32 [4, 72, 1024], P(None, 'lat', 'lon'), may hold values from 0 to 1023
- margin_weight: float32 [4, 72, 1024], P(None, 'lat', 'lon'), may hold values from 0.05 to 0.6
- sea_mask: int32 [72, 1024], P('lat', 'lon'), may hold values 0 or 1
Outputs:
- grad_state: float32 [72, 1024, 128], P('lat', 'lon')
- grad_embed: float32 [16384, 256], P(('lat', 'lon'))
- grad_projection: float32 [256, 128], replicated
- grad_kernel: float32 [7, 7, 128], replicated
- grad_gain: float32 [128], replicated
- grad_w_in: float32 [128, 512], replicated
- grad_w_out: float32 [512, 128], replicated
The draws below stay inside these ranges and needn't reach their ends.
All inputs are finite; a program needn't handle non-finite values. No bound on the sum of `sea_mask` on one device may be relied on, other than what follows from the above.
Results may differ from the reference program's by a relative error of at most 0.0058.
Values may be sent and summed in bfloat16 or wider, within the bound.
No kernel may reach another device: no remote copies, remote signals or barrier semaphores. Data moves between devices by JAX's collectives and lax.ppermute only.
A program may use at most 64 MiB of HBM per device.

```python
import math
import jax
import jax.numpy as jnp
from jax import lax

LAT_DEV = 9
LON_DEV = 256
C = 128
FF = 512
E = 256
A_DEV = 512
TAPS = 7
MARGINS = 4
NLAT = 72
NLON = 1024
A_CELLS = 16384
N_LAT = 8
N_LON = 4


def with_ends(values, own_key, least, high):
    extent = values.shape
    spot = [jax.random.randint(jax.random.fold_in(own_key, axis), (), 0, extent[axis]) for axis in range(len(extent))]
    values = values.at[tuple(spot)].set(least)
    longest = extent.index(max(extent))
    spot[longest] = (spot[longest] + 1) % extent[longest]
    return values.at[tuple(spot)].set(high)


def block_scale(rng, shape, shards, least, high):
    def one(axis_at, parts):
        heights = jax.random.uniform(jax.random.fold_in(jax.random.fold_in(rng, 6), axis_at), (parts,), jnp.float32, least / len(shards), high / len(shards))
        return jnp.repeat(jnp.exp(heights), shape[axis_at] // parts).reshape((-1,) + (1,) * (len(shape) - axis_at - 1))

    level = one(*shards[0])
    for cut in shards[1:]:
        level = level * one(*cut)
    return level


def scatter_about(key, dims, scale, reach, cuts=(), kind=jnp.bfloat16):
    array = jax.random.normal(key, dims, jnp.float32) * scale
    if len(cuts) > 0:
        array = block_scale(key, dims, cuts, -0.22, 0.18) * array
    return jnp.clip(array, min=-reach, max=reach).astype(kind)


def setup_inputs(seed: int = 0) -> dict:
    seeds = jax.random.split(jax.random.key(seed), 12)
    ocean_state = scatter_about(seeds[0], (NLAT, NLON, C), 1.0, 6.0, ((0, 8), (1, 4)))
    cotangent = scatter_about(seeds[1], (NLAT, NLON, C), 1.0, 6.0, ((0, 8), (1, 4)))
    atm_embed = scatter_about(seeds[2], (A_CELLS, E), 1.0, 6.0, ((0, 32),))
    projection = scatter_about(seeds[3], (E, C), E ** -0.5, 0.375)
    dw_kernel = scatter_about(seeds[4], (TAPS, TAPS, C), (TAPS * TAPS) ** -0.5, 0.875, (), jnp.float32)
    norm_gain = jnp.clip(1.0 + 0.15 * jax.random.normal(seeds[5], (C,), jnp.float32), 0.25, 1.75)
    w_in = scatter_about(seeds[6], (C, FF), C ** -0.5, 0.5)
    w_out = scatter_about(seeds[7], (FF, C), FF ** -0.5, 0.25)
    margin_index = with_ends(jax.random.randint(seeds[8], (MARGINS, NLAT, NLON), 0, 2 * A_DEV), jax.random.fold_in(seeds[8], 1), 0, (2 * A_DEV) - 1).astype(jnp.int32)
    margin_weight = jnp.clip(jnp.exp(math.log(0.6) - 2.4849067 * jax.random.uniform(seeds[9], (MARGINS, NLAT, NLON), jnp.float32) ** block_scale(seeds[9], (MARGINS, NLAT, NLON), ((1, 8), (2, 4)), -0.2, 0.2)), 0.05, 0.6)
    sea_mask = with_ends((jax.random.randint(seeds[10], (NLAT, NLON), 0, 4) < 3).astype(jnp.int32), jax.random.fold_in(seeds[10], 1), 0, 1)
    return dict(ocean_state=ocean_state, cotangent=cotangent, atm_embed=atm_embed, projection=projection, dw_kernel=dw_kernel, norm_gain=norm_gain, w_in=w_in, w_out=w_out, margin_index=margin_index, margin_weight=margin_weight, sea_mask=sea_mask)


EPSILON = 1e-05

def wrap_pad(field):
    rows = jnp.pad(field, ((3, 3), (0, 0), (0, 0)))
    return jnp.concatenate([rows[:, -3:], rows, rows[:, :3]], axis=1)

def depthwise(padded, kernel):
    height = padded.shape[0] - 6
    width = padded.shape[1] - 6
    total = jnp.zeros((height, width, padded.shape[2]), jnp.float32)
    for row_tap in range(7):
        for col_tap in range(7):
            total = total + padded[row_tap:row_tap + height, col_tap:col_tap + width] * kernel[row_tap, col_tap]
    return total

def depthwise_back(padded, kernel):
    height = padded.shape[0] - 6
    width = padded.shape[1] - 6
    total = jnp.zeros((height, width, padded.shape[2]), jnp.float32)
    for row_tap in range(7):
        for col_tap in range(7):
            total = total + padded[6 - row_tap:6 - row_tap + height, 6 - col_tap:6 - col_tap + width] * kernel[row_tap, col_tap]
    return total

def kernel_grad(grad, padded):
    height = grad.shape[0]
    width = grad.shape[1]
    pieces = []
    for row_tap in range(7):
        for col_tap in range(7):
            pieces.append(lax.optimization_barrier(jnp.sum(grad * padded[row_tap:row_tap + height, col_tap:col_tap + width], axis=(0, 1))))
    return jnp.stack(pieces).reshape(7, 7, grad.shape[2])

def norm_forward(field):
    center = field - lax.optimization_barrier(jnp.mean(field, axis=-1, keepdims=True))
    sigma = jnp.sqrt(lax.optimization_barrier(jnp.mean(center * center, axis=-1, keepdims=True)) + EPSILON)
    return (center / sigma, sigma)

def norm_back(g_ln, normed, sigma, gain):
    gain_grad = lax.optimization_barrier(jnp.sum(g_ln * normed, axis=(0, 1)))
    g_norm = g_ln * gain
    g_field = (g_norm - lax.optimization_barrier(jnp.mean(g_norm, axis=-1, keepdims=True)) - normed * lax.optimization_barrier(jnp.mean(g_norm * normed, axis=-1, keepdims=True))) / sigma
    return (g_field, gain_grad)

def gelu_tanh(value):
    return jax.nn.gelu(value, approximate=True)

def mlp_back(ln_rows, gy_rows, w_in, w_out):
    pre_act = jnp.dot(ln_rows, w_in, preferred_element_type=jnp.float32)
    hidden, pullback = jax.vjp(gelu_tanh, pre_act)
    hidden = hidden.astype(jnp.bfloat16)
    grad_out = lax.dot_general(hidden, gy_rows, (((0,), (0,)), ((), ())), preferred_element_type=jnp.float32)
    g_hidden = lax.dot_general(gy_rows, w_out, (((1,), (1,)), ((), ())), preferred_element_type=jnp.float32)
    g_pre = pullback(g_hidden)[0].astype(jnp.bfloat16)
    grad_in = lax.dot_general(ln_rows, g_pre, (((0,), (0,)), ((), ())), preferred_element_type=jnp.float32)
    g_ln = lax.dot_general(g_pre, w_in, (((1,), (1,)), ((), ())), preferred_element_type=jnp.float32)
    return (g_ln, grad_in, grad_out)

def global_index(margin_index):
    band = (jnp.arange(NLAT, dtype=jnp.int32) // LAT_DEV)[:, None]
    tile = (jnp.arange(NLON, dtype=jnp.int32) // LON_DEV)[None, :]
    own = (band * N_LON + tile) * A_DEV + margin_index
    following = ((band + 1) * N_LON + tile) * A_DEV + margin_index - A_DEV
    chosen = jnp.where(margin_index < A_DEV, own, following)
    valid = (margin_index < A_DEV) | (band + 1 < N_LAT)
    return jnp.where(valid, chosen, A_CELLS).astype(jnp.int32)

def reference(ocean_state, cotangent, atm_embed, projection, dw_kernel, norm_gain, w_in, w_out, margin_index, margin_weight, sea_mask):
    channels = projection.shape[1]
    targets = global_index(margin_index)
    projected = jnp.dot(atm_embed, projection, preferred_element_type=jnp.float32).astype(jnp.bfloat16)
    projected = lax.optimization_barrier(projected).astype(jnp.float32)
    table = jnp.concatenate([projected, jnp.zeros((1, channels), jnp.float32)], axis=0)
    forcing = jnp.zeros((NLAT, NLON, channels), jnp.float32)
    for slot in range(MARGINS):
        forcing = forcing + margin_weight[slot][..., None] * table[targets[slot]]
    field = ocean_state.astype(jnp.float32) + forcing
    padded = wrap_pad(field)
    conv_out = depthwise(padded, dw_kernel)
    normed, sigma = norm_forward(conv_out)
    ln_cells = (normed * norm_gain).astype(jnp.bfloat16)
    g_out = cotangent.astype(jnp.float32)
    gy_cells = (sea_mask.astype(jnp.float32)[..., None] * g_out).astype(jnp.bfloat16)
    blocks = N_LAT * N_LON
    size_block = LAT_DEV * LON_DEV

    def one_block(pair):
        return mlp_back(pair[0], pair[1], w_in, w_out)
    g_ln, grad_in, grad_out = lax.map(one_block, (ln_cells.reshape(blocks, size_block, channels), gy_cells.reshape(blocks, size_block, channels)))
    g_ln = g_ln.reshape(NLAT, NLON, channels)
    g_conv, grad_gain = norm_back(g_ln, normed, sigma, norm_gain)
    grad_kernel = kernel_grad(g_conv, padded)
    grad_state = g_out + depthwise_back(wrap_pad(g_conv), dw_kernel)
    g_table = jnp.zeros((A_CELLS + 1, channels), jnp.float32)
    for slot in range(MARGINS):
        g_table = g_table.at[targets[slot].reshape(-1)].add((margin_weight[slot][..., None] * grad_state).reshape(-1, channels))
    g_projected = g_table[:A_CELLS]
    grad_embed = jnp.dot(g_projected, projection.astype(jnp.float32).T, precision=lax.Precision.HIGHEST)
    grad_projection = jnp.dot(atm_embed.astype(jnp.float32).T, g_projected, precision=lax.Precision.HIGHEST)
    return (grad_state, grad_embed, grad_projection, grad_kernel, grad_gain, lax.optimization_barrier(jnp.sum(grad_in, axis=0)), lax.optimization_barrier(jnp.sum(grad_out, axis=0)))
```

```python
import jax
import jax.numpy as jnp
from jax import lax
from jax.sharding import PartitionSpec as P

EPSILON = 1e-05


def shifted(x, axis, by):
    size = lax.axis_size(axis)
    pairs = [(i, i + by) for i in range(size) if 0 <= i + by < size]
    return lax.ppermute(x, axis, pairs)


def xor_swap(x, axis, mask):
    size = lax.axis_size(axis)
    return lax.ppermute(x, axis, [(i, i ^ mask) for i in range(size)])


def masks(axis):
    size = lax.axis_size(axis)
    if size & (size - 1):
        return None
    return [1 << k for k in range(size.bit_length() - 1)]


def fold(value, axis, chosen):
    for mask in chosen:
        mine = value.astype(jnp.bfloat16)
        other = xor_swap(mine, axis, mask)
        value = mine.astype(jnp.float32) + other.astype(jnp.float32)
    return value


def sum_over_mesh(value):
    for axis in ("lat", "lon"):
        steps = masks(axis)
        value = lax.psum(value, axis) if steps is None else fold(value, axis, steps)
    return value


def sum_pair_over_mesh(first, second):
    steps = masks("lat")
    if not steps or masks("lon") is None:
        return lax.psum((first, second), ("lat", "lon"))
    odd = lax.rem(lax.axis_index("lat"), 2) == 1
    first, second = first.astype(jnp.bfloat16), second.astype(jnp.bfloat16)
    kept = jnp.where(odd, second, first)
    given = xor_swap(jnp.where(odd, first, second), "lat", 1)
    value = kept.astype(jnp.float32) + given.astype(jnp.float32)
    value = fold(value, "lat", steps[1:])
    value = fold(value, "lon", masks("lon"))
    mine = value.astype(jnp.bfloat16)
    other = xor_swap(mine, "lat", 1)
    low = jnp.where(odd, other, mine).astype(jnp.float32)
    high = jnp.where(odd, mine, other).astype(jnp.float32)
    return low, high


def with_halo(block, sides, width):
    for axis, dim in sides:
        count = lax.axis_size(axis)
        forward = [(i, i + 1) for i in range(count - 1)]
        forward.append((count - 1, 0))
        backward = [(target, source) for source, target in forward]
        rims = (
            lax.slice_in_dim(block, block.shape[dim] - width, None, axis=dim).astype(jnp.bfloat16),
            lax.slice_in_dim(block, 0, width, axis=dim).astype(jnp.bfloat16),
        )
        low = lax.ppermute(rims[0], axis, forward).astype(jnp.float32)
        high = lax.ppermute(rims[1], axis, backward).astype(jnp.float32)
        block = jnp.concatenate([low, block, high], axis=dim)
    return block


def depthwise(padded, kernel):
    height = padded.shape[0] - 6
    width = padded.shape[1] - 6
    total = jnp.zeros((height, width, padded.shape[2]), jnp.float32)
    for row_tap in range(7):
        for col_tap in range(7):
            total = (
                total
                + padded[row_tap : row_tap + height, col_tap : col_tap + width]
                * kernel[row_tap, col_tap]
            )
    return total


def depthwise_back(padded, kernel):
    height = padded.shape[0] - 6
    width = padded.shape[1] - 6
    total = jnp.zeros((height, width, padded.shape[2]), jnp.float32)
    for row_tap in range(7):
        for col_tap in range(7):
            total = (
                total
                + padded[6 - row_tap : 6 - row_tap + height, 6 - col_tap : 6 - col_tap + width]
                * kernel[row_tap, col_tap]
            )
    return total


def kernel_grad(grad, padded):
    height = grad.shape[0]
    width = grad.shape[1]
    pieces = []
    for row_tap in range(7):
        for col_tap in range(7):
            pieces.append(
                jnp.sum(
                    grad * padded[row_tap : row_tap + height, col_tap : col_tap + width],
                    axis=(0, 1),
                )
            )
    return jnp.stack(pieces).reshape(7, 7, grad.shape[2])


def norm_forward(field):
    center = field - jnp.mean(field, axis=-1, keepdims=True)
    sigma = jnp.sqrt(jnp.mean(center * center, axis=-1, keepdims=True) + EPSILON)
    return (center / sigma, sigma)


def norm_back(g_ln, normed, sigma, gain):
    gain_grad = jnp.sum(g_ln * normed, axis=(0, 1))
    g_norm = g_ln * gain
    g_field = (
        g_norm
        - jnp.mean(g_norm, axis=-1, keepdims=True)
        - normed * jnp.mean(g_norm * normed, axis=-1, keepdims=True)
    ) / sigma
    return (g_field, gain_grad)


def gelu_tanh(value):
    return jax.nn.gelu(value, approximate=True)


def mlp_back(ln_rows, gy_rows, w_in, w_out):
    pre_act = jnp.dot(ln_rows, w_in, preferred_element_type=jnp.float32)
    hidden, pullback = jax.vjp(gelu_tanh, pre_act)
    hidden = hidden.astype(jnp.bfloat16)
    grad_out = lax.dot_general(
        gy_rows, hidden, (((0,), (0,)), ((), ())), preferred_element_type=jnp.float32
    )
    g_hidden = lax.dot_general(
        gy_rows, w_out, (((1,), (1,)), ((), ())), preferred_element_type=jnp.float32
    )
    g_pre = pullback(g_hidden)[0].astype(jnp.bfloat16)
    grad_in = lax.dot_general(
        ln_rows, g_pre, (((0,), (0,)), ((), ())), preferred_element_type=jnp.float32
    )
    g_ln = lax.dot_general(
        g_pre, w_in, (((1,), (1,)), ((), ())), preferred_element_type=jnp.float32
    )
    return (g_ln, grad_in, grad_out)


def clear_ends(padded):
    band = lax.axis_index("lat")
    bands = lax.axis_size("lat")
    position = jnp.arange(padded.shape[0], dtype=jnp.int32)
    dropped = (band == 0) & (position < 3) | (band == bands - 1) & (position >= padded.shape[0] - 3)
    return padded * jnp.where(dropped, 0.0, 1.0).astype(jnp.float32)[:, None, None]


def margin_block(index_rows, weight_rows, slots):
    columns = jnp.arange(slots, dtype=jnp.int32)[None, :]
    dense = jnp.zeros((index_rows.shape[1], slots), jnp.float32)
    for slot in range(index_rows.shape[0]):
        dense = dense + jnp.where(
            index_rows[slot][:, None] == columns, weight_rows[slot][:, None], 0.0
        )
    return dense


def block_rows(height, width):
    limit = max(1, 2048 // width)
    best = 1
    for count in range(1, height + 1):
        if height % count == 0 and count <= limit:
            best = count
    return best


def shards(
    ocean_state,
    cotangent,
    atm_embed,
    projection,
    dw_kernel,
    norm_gain,
    w_in,
    w_out,
    margin_index,
    margin_weight,
    sea_mask,
):
    cells_atm = atm_embed.shape[0]
    channels = projection.shape[1]
    height = ocean_state.shape[0]
    width = ocean_state.shape[1]
    margins = margin_index.shape[0]
    slots = 2 * cells_atm
    group = block_rows(height, width) * width
    blocks = height * width // group
    index_blocks = jnp.transpose(margin_index.reshape(margins, blocks, group), (1, 0, 2))
    weight_blocks = jnp.transpose(margin_weight.reshape(margins, blocks, group), (1, 0, 2))
    next_embed = shifted(atm_embed, "lat", -1)
    window_embed = jnp.concatenate([atm_embed, next_embed], axis=0)
    window = jnp.dot(window_embed, projection, preferred_element_type=jnp.float32).astype(
        jnp.bfloat16
    )
    window = lax.optimization_barrier(window).astype(jnp.float32)

    def forward_block(pair):
        dense = margin_block(pair[0], pair[1], slots)
        return jnp.dot(dense, window, precision=lax.Precision.HIGHEST)

    forcing = lax.map(forward_block, (index_blocks, weight_blocks)).reshape(height, width, channels)
    field = ocean_state.astype(jnp.float32) + forcing
    padded = clear_ends(with_halo(field, (("lon", 1), ("lat", 0)), 3))
    conv_out = depthwise(padded, dw_kernel)
    normed, sigma = norm_forward(conv_out)
    ln_cells = (normed * norm_gain).astype(jnp.bfloat16)
    g_out = cotangent.astype(jnp.float32)
    gy_cells = (sea_mask.astype(jnp.float32)[..., None] * g_out).astype(jnp.bfloat16)
    g_ln, grad_in, grad_out = mlp_back(
        ln_cells.reshape(-1, channels), gy_cells.reshape(-1, channels), w_in, w_out
    )
    grad_in, grad_out = sum_pair_over_mesh(grad_in, grad_out)
    g_conv, grad_gain = norm_back(g_ln.reshape(height, width, channels), normed, sigma, norm_gain)
    grad_kernel = kernel_grad(g_conv, padded)
    g_padded = clear_ends(with_halo(g_conv, (("lon", 1), ("lat", 0)), 3))
    grad_state = g_out + depthwise_back(g_padded, dw_kernel)
    state_blocks = grad_state.reshape(blocks, group, channels)

    def backward_block(total, triple):
        dense = margin_block(triple[0], triple[1], slots)
        added = lax.dot_general(
            dense,
            triple[2],
            (((0,), (0,)), ((), ())),
            precision=lax.Precision.HIGHEST,
            preferred_element_type=jnp.float32,
        )
        return (total + added, None)

    g_window, unused = lax.scan(
        backward_block,
        jnp.zeros((slots, channels), jnp.float32),
        (index_blocks, weight_blocks, state_blocks),
    )
    g_window_embed = jnp.dot(
        g_window, projection.astype(jnp.float32).T, precision=lax.Precision.HIGHEST
    )
    returned = shifted(g_window_embed[cells_atm:], "lat", 1)
    grad_embed = g_window_embed[:cells_atm] + returned
    grad_projection = jnp.dot(
        window_embed.astype(jnp.float32).T, g_window, precision=lax.Precision.HIGHEST
    )
    taps = grad_kernel.shape[0] * grad_kernel.shape[1]
    late = jnp.concatenate(
        [grad_projection, grad_kernel.reshape(taps, channels), grad_gain[None]], axis=0
    )
    late = sum_over_mesh(late)
    rows = projection.shape[0]
    return (
        grad_state,
        grad_embed,
        late[:rows],
        late[rows : rows + taps].reshape(grad_kernel.shape),
        late[rows + taps],
        grad_in,
        grad_out.T,
    )


def solution(mesh):
    return jax.shard_map(
        shards,
        mesh=mesh,
        in_specs=(
            P("lat", "lon", None),
            P("lat", "lon", None),
            P(("lat", "lon"), None),
            P(),
            P(),
            P(),
            P(),
            P(),
            P(None, "lat", "lon"),
            P(None, "lat", "lon"),
            P("lat", "lon"),
        ),
        out_specs=(P("lat", "lon", None), P(("lat", "lon"), None), P(), P(), P(), P(), P()),
        check_vma=False,
    )
```

```python
import functools
import jax
import jax.numpy as jnp
from jax import lax
from jax.experimental import pallas as pl
from jax.experimental.pallas import tpu as pltpu
from jax.sharding import PartitionSpec as P

EPSILON = 1e-05
ROOT = 0.7978845608028654
CUBIC = 0.044715
ROWS = 128
EDGE = 8
LIMIT = 20 << 20
bf16 = jnp.bfloat16
f32 = jnp.float32


def kernel_call(body, outs, scratch, args, name, flops, nbytes):
    vmem = pl.BlockSpec(memory_space=pltpu.VMEM)
    return pl.pallas_call(
        body,
        in_specs=[vmem] * len(args),
        out_specs=[vmem] * len(outs),
        out_shape=[jax.ShapeDtypeStruct(shape, dtype) for shape, dtype in outs],
        scratch_shapes=[pltpu.VMEM(shape, dtype) for shape, dtype in scratch],
        compiler_params=pltpu.CompilerParams(vmem_limit_bytes=LIMIT),
        cost_estimate=pl.CostEstimate(flops=flops, bytes_accessed=nbytes, transcendentals=0),
        name=name,
    )(*args)


def merged_margins(index, weight):
    merged = []
    for slot in range(len(index)):
        total = weight[slot]
        for before in range(slot):
            total = total + jnp.where(index[before] == index[slot], weight[before], 0.0)
        merged.append(total.astype(bf16))
    return merged


def dense_block(index, weight, block, places):
    dense = jnp.zeros(places.shape, bf16)
    for slot in range(len(index)):
        place = jnp.where(index[slot] // ROWS == block, index[slot] % ROWS, -1)
        place = jnp.broadcast_to(place.astype(f32).astype(bf16), places.shape)
        dense = jnp.where(places == place, jnp.broadcast_to(weight[slot], places.shape), dense)
    return dense


def margins_kernel(index_ref, weight_ref, window_ref, dense_ref, part_ref):
    margins, height, width = index_ref.shape
    own = window_ref.shape[1]
    places = lax.broadcasted_iota(jnp.int32, (ROWS, width), 0).astype(f32).astype(bf16)

    @pl.loop(0, height)
    def _(row):
        index = [index_ref[slot, pl.ds(row, 1), :] for slot in range(margins)]
        weight = [weight_ref[slot, pl.ds(row, 1), :] for slot in range(margins)]
        weight = merged_margins(index, weight)
        cells = pl.ds(pl.multiple_of(row * width, width), width)
        for block in range(dense_ref.shape[0] // ROWS):
            dense_ref[block * ROWS : (block + 1) * ROWS, cells] = dense_block(
                index, weight, block, places
            )
        part = jnp.dot(window_ref[...], dense_ref[:own, cells], preferred_element_type=f32)
        part_ref[row] = part.T


def field_kernel(dense_ref, window_ref, part_ref, state_ref, field_ref, side_ref, end_ref):
    height, width, channels = field_ref.shape
    own = window_ref.shape[1]

    @pl.loop(0, height)
    def _(row):
        cells = pl.ds(pl.multiple_of(row * width, width), width)
        part = jnp.dot(window_ref[...], dense_ref[own:, cells], preferred_element_type=f32)
        field = state_ref[row].astype(f32) + (part_ref[row] + part.T)
        field_ref[row] = field
        side_ref[0, row] = field[width - EDGE :].astype(bf16)
        side_ref[1, row] = field[:EDGE].astype(bf16)

    end_ref[0] = field_ref[height - 3 :].astype(bf16)
    end_ref[1] = field_ref[:3].astype(bf16)


def spread(kernel_ref, spread_ref, flip):
    taps = kernel_ref.shape[0]
    for row in range(taps):
        for col in range(taps):
            source = kernel_ref[row, col : col + 1, :]
            place = (taps - 1 - row) * taps + taps - 1 - col if flip else row * taps + col
            spread_ref[place] = jnp.broadcast_to(source, (8, source.shape[1]))


def tap_sums(sums, rows, load, spread_ref):
    taps = 7
    for col_tap in range(taps):
        for row in rows:
            value = None
            for row_tap in range(taps):
                out = row - row_tap
                if 0 <= out < len(sums):
                    value = load(row, col_tap) if value is None else value
                    term = value * spread_ref[row_tap * taps + col_tap]
                    sums[out] = term if sums[out] is None else sums[out] + term


def local_taps(padded_ref, spread_ref, out_ref):
    height, width, channels = out_ref.shape

    @pl.loop(0, width // 8)
    def _(block):
        col = pl.multiple_of(block * 8, 8)
        sums = [None] * height

        def load(row, tap):
            return padded_ref[row - 3, pl.ds(col + (tap + EDGE - 3), 8), :]

        tap_sums(sums, range(3, height + 3), load, spread_ref)
        for row in range(height):
            out_ref[row, pl.ds(col, 8), :] = sums[row]


def pad_cols(source_ref, padded_ref):
    height, width, channels = source_ref.shape
    padded_ref[:, :EDGE, :] = jnp.zeros((height, EDGE, channels), f32)
    padded_ref[:, EDGE + width :, :] = jnp.zeros((height, EDGE, channels), f32)
    padded_ref[:, EDGE : EDGE + width, :] = source_ref[...]


def rest_taps(base_ref, left_ref, right_ref, low_ref, high_ref, spread_ref, out_ref, strip, ends):
    height, width, channels = base_ref.shape
    strip[...] = jnp.zeros(strip.shape, f32)
    strip[0, :, :EDGE, :] = left_ref[...].astype(f32)
    strip[1, :, 2 * EDGE :, :] = right_ref[...].astype(f32)
    ends[0:3] = low_ref[...].astype(f32)
    ends[3:6] = high_ref[...].astype(f32)

    @pl.loop(0, width // 8)
    def _(block):
        col = pl.multiple_of(block * 8, 8)
        sums = [base_ref[row, pl.ds(col, 8), :] for row in range(height)]

        def load(row, tap):
            place = row if row < 3 else row - height
            return ends[place, pl.ds(col + (tap + EDGE - 3), 8), :]

        tap_sums(sums, (0, 1, 2, height + 3, height + 4, height + 5), load, spread_ref)
        for row in range(height):
            out_ref[row, pl.ds(col, 8), :] = sums[row]

    @pl.loop(0, 2)
    def _(side):
        col = pl.multiple_of(side * (width - 8), 8)
        sums = [out_ref[row, pl.ds(col, 8), :] for row in range(height)]

        def load(row, tap):
            return strip[side, row - 3, pl.ds(tap + EDGE - 3, 8), :]

        tap_sums(sums, range(3, height + 3), load, spread_ref)
        for row in range(height):
            out_ref[row, pl.ds(col, 8), :] = sums[row]


def conv_kernel(field_ref, kernel_ref, out_ref, padded, weights):
    spread(kernel_ref, weights, False)
    pad_cols(field_ref, padded)
    local_taps(padded, weights, out_ref)


def mlp_kernel(
    base_ref,
    field_ref,
    left_ref,
    right_ref,
    low_ref,
    high_ref,
    kernel_ref,
    cotangent_ref,
    mask_ref,
    gain_ref,
    w_in_ref,
    w_out_ref,
    w_in_t_ref,
    w_out_t_ref,
    g_ref,
    padded_ref,
    pair_ref,
    gain_out_ref,
    side_ref,
    end_ref,
    conv,
    weights,
    strip,
    ends,
):
    height, width, channels = base_ref.shape
    spread(kernel_ref, weights, False)
    rest_taps(base_ref, left_ref, right_ref, low_ref, high_ref, weights, conv, strip, ends)
    padded_ref[3 : 3 + height, EDGE : EDGE + width, :] = field_ref[...]
    padded_ref[3 : 3 + height, :EDGE, :] = strip[0, :, :EDGE, :]
    padded_ref[3 : 3 + height, EDGE + width :, :] = strip[1, :, 2 * EDGE :, :]
    padded_ref[:3] = ends[0:3]
    padded_ref[3 + height :] = ends[3:6]
    pair_ref[...] = jnp.zeros(pair_ref.shape, f32)
    gain_out_ref[...] = jnp.zeros(gain_out_ref.shape, f32)
    gain = gain_ref[...]

    @pl.loop(0, height)
    def _(row):
        value = conv[row]
        center = value - jnp.mean(value, axis=-1, keepdims=True)
        scale = lax.rsqrt(jnp.mean(center * center, axis=-1, keepdims=True) + EPSILON)
        normed = center * scale
        ln_rows = (normed * gain).astype(bf16)
        mask = jnp.broadcast_to(mask_ref[pl.ds(row, 1), :].astype(f32), (channels, width)).T
        gy_rows = (mask * cotangent_ref[row].astype(f32)).astype(bf16)
        pre = jnp.dot(ln_rows, w_in_ref[...], preferred_element_type=f32)
        g_hidden = jnp.dot(gy_rows, w_out_t_ref[...], preferred_element_type=f32)
        square = pre * pre
        half = 0.5 + 0.5 * jnp.tanh(pre * (ROOT + (ROOT * CUBIC) * square))
        hidden = pre * half
        slope = half + hidden * (1.0 - half) * (2 * ROOT + (6 * ROOT * CUBIC) * square)
        g_pre = (g_hidden * slope).astype(bf16)
        hidden = hidden.astype(bf16)
        pair_ref[0] += lax.dot_general(
            ln_rows, g_pre, (((0,), (0,)), ((), ())), preferred_element_type=f32
        )
        pair_ref[1] += lax.dot_general(
            gy_rows, hidden, (((0,), (0,)), ((), ())), preferred_element_type=f32
        )
        g_ln = jnp.dot(g_pre, w_in_t_ref[...], preferred_element_type=f32)
        gain_out_ref[...] += jnp.sum((g_ln * normed).reshape(width // 8, 8, channels), axis=0)
        g_norm = g_ln * gain
        g_conv = (
            g_norm
            - jnp.mean(g_norm, axis=-1, keepdims=True)
            - normed * jnp.mean(g_norm * normed, axis=-1, keepdims=True)
        ) * scale
        g_ref[row] = g_conv
        side_ref[0, row] = g_conv[width - EDGE :].astype(bf16)
        side_ref[1, row] = g_conv[:EDGE].astype(bf16)

    end_ref[0] = g_ref[height - 3 :].astype(bf16)
    end_ref[1] = g_ref[:3].astype(bf16)


def grads_kernel(g_ref, field_ref, kernel_ref, grad_ref, out_ref, padded, weights):
    height, width, channels = g_ref.shape
    taps = kernel_ref.shape[0]
    for col_tap in range(taps):

        def body(block, sums):
            sums = list(sums)
            col = pl.multiple_of(block * 8, 8)
            g_rows = [g_ref[row, pl.ds(col, 8), :] for row in range(height)]
            for row in range(height + taps - 1):
                value = field_ref[row, pl.ds(col + (col_tap + EDGE - 3), 8), :]
                for row_tap in range(taps):
                    if 0 <= row - row_tap < height:
                        sums[row_tap] = sums[row_tap] + g_rows[row - row_tap] * value
            return tuple(sums)

        start = tuple(jnp.zeros((8, channels), f32) for _ in range(taps))
        sums = lax.fori_loop(0, width // 8, body, start)
        for row_tap in range(taps):
            place = row_tap * taps + col_tap
            grad_ref[place : place + 1, :] = jnp.sum(sums[row_tap], axis=0, keepdims=True)
    spread(kernel_ref, weights, True)
    pad_cols(g_ref, padded)
    local_taps(padded, weights, out_ref)


def state_kernel(
    base_ref,
    left_ref,
    right_ref,
    low_ref,
    high_ref,
    kernel_ref,
    cotangent_ref,
    dense_ref,
    state_ref,
    window_ref,
    weights,
    strip,
    ends,
    sums,
    halves,
):
    height, width, channels = base_ref.shape
    spread(kernel_ref, weights, True)
    rest_taps(base_ref, left_ref, right_ref, low_ref, high_ref, weights, sums, strip, ends)

    @pl.loop(0, height)
    def _(row):
        state = cotangent_ref[row].astype(f32) + sums[row]
        state_ref[row] = state
        high = state.astype(bf16)
        cells = pl.ds(pl.multiple_of(row * width, width), width)
        halves[cells, :channels] = high
        halves[cells, channels:] = (state - high.astype(f32)).astype(bf16)

    @pl.loop(0, window_ref.shape[0] // 256)
    def _(block):
        slots = pl.ds(pl.multiple_of(block * 256, 256), 256)
        both = jnp.dot(dense_ref[slots, :], halves[...], preferred_element_type=f32)
        window_ref[slots, :] = both[:, :channels] + both[:, channels:]


def shifted(x, axis, by, wrap=False):
    size = lax.axis_size(axis)
    pairs = [(i, (i + by) % size) for i in range(size) if wrap or 0 <= i + by < size]
    return lax.ppermute(x, axis, pairs)


def exchange(side, end):
    left = shifted(side[0], "lon", 1, True)
    right = shifted(side[1], "lon", -1, True)
    height = left.shape[0]
    to_high = jnp.concatenate([left[height - 3 :], end[0], right[height - 3 :]], axis=1)
    to_low = jnp.concatenate([left[:3], end[1], right[:3]], axis=1)
    low = shifted(to_high, "lat", 1)
    high = shifted(to_low, "lat", -1)
    return left, right, low, high


def xor_swap(x, axis, mask):
    size = lax.axis_size(axis)
    return lax.ppermute(x, axis, [(i, i ^ mask) for i in range(size)])


def masks(axis):
    size = lax.axis_size(axis)
    if size & (size - 1):
        return None
    return [1 << k for k in range(size.bit_length() - 1)]


def fold(value, axis, chosen, dtype=bf16):
    for mask in chosen:
        mine = value.astype(dtype)
        other = xor_swap(mine, axis, mask)
        value = mine.astype(f32) + other.astype(f32)
    return value


def sum_over_mesh(value):
    for axis in ("lat", "lon"):
        steps = masks(axis)
        value = lax.psum(value, axis) if steps is None else fold(value, axis, steps, f32)
    return value


def sum_pair_over_mesh(pair):
    steps = masks("lat")
    if not steps or masks("lon") is None:
        return lax.psum(pair, ("lat", "lon"))
    odd = lax.rem(lax.axis_index("lat"), 2) == 1
    kept = jnp.where(odd, pair[1], pair[0])
    given = xor_swap(jnp.where(odd, pair[0], pair[1]), "lat", 1)
    value = kept + given
    value = fold(value, "lat", steps[1:])
    value = fold(value, "lon", masks("lon"))
    other = xor_swap(value, "lat", 1)
    return jnp.where(odd, other, value), jnp.where(odd, value, other)


def shards(
    ocean_state,
    cotangent,
    atm_embed,
    projection,
    dw_kernel,
    norm_gain,
    w_in,
    w_out,
    margin_index,
    margin_weight,
    sea_mask,
):
    cells_atm = atm_embed.shape[0]
    channels = projection.shape[1]
    height, width = ocean_state.shape[:2]
    taps = dw_kernel.shape[0]
    hidden = w_in.shape[1]
    slots = 2 * cells_atm
    cells = height * width
    grid = (height, width, channels)
    wide = width + 2 * EDGE
    tap_scratch = ((taps * taps, 8, channels), f32)
    strip = ((2, height, 3 * EDGE, channels), f32)
    ends = ((6, wide, channels), f32)
    own = lax.dot_general(
        projection, atm_embed, (((0,), (1,)), ((), ())), preferred_element_type=f32
    ).astype(bf16)
    following = shifted(own, "lat", -1)
    next_embed = shifted(atm_embed, "lat", -1)
    dense, part = kernel_call(
        margins_kernel,
        [((slots, cells), bf16), (grid, f32)],
        [],
        (margin_index, margin_weight, own),
        "margins",
        2 * cells * cells_atm * channels,
        8 << 20,
    )
    field, side, end = kernel_call(
        field_kernel,
        [(grid, f32), ((2, height, EDGE, channels), bf16), ((2, 3, width, channels), bf16)],
        [],
        (dense, following, part, ocean_state),
        "field",
        2 * cells * cells_atm * channels,
        8 << 20,
    )
    left, right, low, high = exchange(side, end)
    (conv,) = kernel_call(
        conv_kernel,
        [(grid, f32)],
        [((height, wide, channels), f32), tap_scratch],
        (field, dw_kernel),
        "conv",
        cells * channels * 98,
        16 << 20,
    )
    g_conv, padded, pair, gain_rows, side, end = kernel_call(
        mlp_kernel,
        [
            (grid, f32),
            ((height + 6, wide, channels), f32),
            ((2, channels, hidden), f32),
            ((8, channels), f32),
            ((2, height, EDGE, channels), bf16),
            ((2, 3, width, channels), bf16),
        ],
        [(grid, f32), tap_scratch, strip, ends],
        (
            conv,
            field,
            left,
            right,
            low,
            high,
            dw_kernel,
            cotangent,
            sea_mask,
            norm_gain[None],
            w_in,
            w_out,
            w_in.T,
            w_out.T,
        ),
        "mlp",
        cells * channels * hidden * 10,
        32 << 20,
    )
    left, right, low, high = exchange(side, end)
    grad_in, grad_out = sum_pair_over_mesh(pair)
    grad_kernel, back = kernel_call(
        grads_kernel,
        [((taps * taps, channels), f32), (grid, f32)],
        [((height, wide, channels), f32), tap_scratch],
        (g_conv, padded, dw_kernel),
        "grads",
        cells * channels * 196,
        32 << 20,
    )
    grad_state, g_window = kernel_call(
        state_kernel,
        [(grid, f32), ((slots, channels), f32)],
        [tap_scratch, strip, ends, (grid, f32), ((cells, 2 * channels), bf16)],
        (back, left, right, low, high, dw_kernel, cotangent, dense),
        "state",
        cells * slots * channels * 4,
        16 << 20,
    )
    returned = shifted(g_window[cells_atm:].astype(bf16), "lat", 1)
    grad_projection = lax.dot_general(
        jnp.concatenate([atm_embed, next_embed], axis=0),
        g_window.astype(bf16),
        (((0,), (0,)), ((), ())),
        preferred_element_type=f32,
    )
    late = jnp.concatenate(
        [grad_projection, grad_kernel, jnp.sum(gain_rows, axis=0)[None]], axis=0
    )
    late = sum_over_mesh(late)
    g_projected = (g_window[:cells_atm] + returned.astype(f32)).astype(bf16)
    grad_embed = lax.dot_general(
        g_projected, projection, (((1,), (1,)), ((), ())), preferred_element_type=f32
    )
    rows = projection.shape[0]
    return (
        grad_state,
        grad_embed,
        late[:rows],
        late[rows : rows + taps * taps].reshape(dw_kernel.shape),
        late[rows + taps * taps],
        grad_in,
        grad_out.T,
    )


def solution(mesh):
    return jax.shard_map(
        shards,
        mesh=mesh,
        in_specs=(
            P("lat", "lon", None),
            P("lat", "lon", None),
            P(("lat", "lon"), None),
            P(),
            P(),
            P(),
            P(),
            P(),
            P(None, "lat", "lon"),
            P(None, "lat", "lon"),
            P("lat", "lon"),
        ),
        out_specs=(P("lat", "lon", None), P(("lat", "lon"), None), P(), P(), P(), P(), P()),
        check_vma=False,
    )
```

```python
import functools
import jax
import jax.numpy as jnp
from jax import lax
from jax.experimental import pallas as pl
from jax.experimental.pallas import tpu as pltpu
from jax.sharding import PartitionSpec as P

EPSILON = 1e-05
ROOT = 0.7978845608028654
CUBIC = 0.044715
ROWS = 128
EDGE = 8
LIMIT = 20 << 20
bf16 = jnp.bfloat16
f32 = jnp.float32


def kernel_call(body, outs, scratch, args, flops, nbytes):
    vmem = pl.BlockSpec(memory_space=pltpu.VMEM)
    return pl.pallas_call(
        body,
        in_specs=[vmem] * len(args),
        out_specs=[vmem] * len(outs),
        out_shape=[jax.ShapeDtypeStruct(shape, dtype) for shape, dtype in outs],
        scratch_shapes=[pltpu.VMEM(shape, dtype) for shape, dtype in scratch],
        compiler_params=pltpu.CompilerParams(vmem_limit_bytes=LIMIT),
        cost_estimate=pl.CostEstimate(flops=flops, bytes_accessed=nbytes, transcendentals=0),
    )(*args)


def merged_margins(index, weight):
    merged = []
    for slot in range(len(index)):
        total = weight[slot]
        for before in range(slot):
            total = total + jnp.where(index[before] == index[slot], weight[before], 0.0)
        merged.append(total.astype(bf16))
    return merged


def dense_block(index, weight, block, places):
    dense = jnp.zeros(places.shape, bf16)
    for slot in range(len(index)):
        place = jnp.where(index[slot] // ROWS == block, index[slot] % ROWS, -1)
        place = jnp.broadcast_to(place.astype(f32).astype(bf16), places.shape)
        dense = jnp.where(places == place, jnp.broadcast_to(weight[slot], places.shape), dense)
    return dense


def margins_kernel(index_ref, weight_ref, window_ref, dense_ref, part_ref):
    height, margins, width = index_ref.shape
    own = window_ref.shape[1]
    places = lax.broadcasted_iota(jnp.int32, (ROWS, width), 0).astype(f32).astype(bf16)

    @pl.loop(0, height)
    def _(row):
        index = [index_ref[row, slot : slot + 1, :] for slot in range(margins)]
        weight = [weight_ref[row, slot : slot + 1, :] for slot in range(margins)]
        weight = merged_margins(index, weight)
        cells = pl.ds(pl.multiple_of(row * width, width), width)
        for block in range(dense_ref.shape[0] // ROWS):
            dense_ref[block * ROWS : (block + 1) * ROWS, cells] = dense_block(
                index, weight, block, places
            )
        part = jnp.dot(window_ref[...], dense_ref[:own, cells], preferred_element_type=f32)
        part_ref[row] = part.T


def field_kernel(dense_ref, window_ref, part_ref, state_ref, field_ref, side_ref, end_ref):
    height, width, _ = field_ref.shape
    own = window_ref.shape[1]

    @pl.loop(0, height)
    def _(row):
        cells = pl.ds(pl.multiple_of(row * width, width), width)
        part = jnp.dot(window_ref[...], dense_ref[own:, cells], preferred_element_type=f32)
        field = state_ref[row].astype(f32) + (part_ref[row] + part.T)
        field_ref[row] = field
        side_ref[0, row] = field[width - EDGE :].astype(bf16)
        side_ref[1, row] = field[:EDGE].astype(bf16)

    end_ref[0] = field_ref[height - 3 :].astype(bf16)
    end_ref[1] = field_ref[:3].astype(bf16)


def spread(kernel_ref, spread_ref, flip):
    taps = kernel_ref.shape[0]
    for row in range(taps):
        for col in range(taps):
            source = kernel_ref[row, col : col + 1, :]
            place = (taps - 1 - row) * taps + taps - 1 - col if flip else row * taps + col
            spread_ref[place] = jnp.broadcast_to(source, (8, source.shape[1]))


def tap_sums(sums, rows, load, spread_ref):
    taps = 7
    for col_tap in range(taps):
        for row in rows:
            value = None
            for row_tap in range(taps):
                out = row - row_tap
                if 0 <= out < len(sums):
                    value = load(row, col_tap) if value is None else value
                    term = value * spread_ref[row_tap * taps + col_tap]
                    sums[out] = term if sums[out] is None else sums[out] + term


def local_taps(padded_ref, spread_ref, out_ref, start=0):
    height, width, _ = out_ref.shape

    @pl.loop(0, width // 8)
    def _(block):
        col = pl.multiple_of(block * 8, 8)
        sums = [None] * height

        def load(row, tap):
            return padded_ref[row - 3, pl.ds(col + (start + tap + EDGE - 3), 8), :]

        tap_sums(sums, range(3, height + 3), load, spread_ref)
        for row in range(height):
            out_ref[row, pl.ds(col, 8), :] = sums[row]


def pad_cols(source_ref, padded_ref):
    height, width, channels = source_ref.shape
    padded_ref[:, :EDGE, :] = jnp.zeros((height, EDGE, channels), f32)
    padded_ref[:, EDGE + width :, :] = jnp.zeros((height, EDGE, channels), f32)
    padded_ref[:, EDGE : EDGE + width, :] = source_ref[...]


def rest_taps(base_refs, left_ref, right_ref, low_ref, high_ref, spread_ref, out_ref, strip, ends):
    height, width, _ = out_ref.shape
    strip[...] = jnp.zeros(strip.shape, f32)
    strip[0, :, :EDGE, :] = left_ref[...].astype(f32)
    strip[1, :, 2 * EDGE :, :] = right_ref[...].astype(f32)
    ends[0:3] = low_ref[...].astype(f32)
    ends[3:6] = high_ref[...].astype(f32)

    def part(base_ref, start):
        @pl.loop(0, base_ref.shape[1] // 8)
        def _(block):
            col = pl.multiple_of(block * 8, 8)
            sums = [base_ref[row, pl.ds(col, 8), :] for row in range(height)]

            def load(row, tap):
                place = row if row < 3 else row - height
                return ends[place, pl.ds(col + (start + tap + EDGE - 3), 8), :]

            tap_sums(sums, (0, 1, 2, height + 3, height + 4, height + 5), load, spread_ref)
            for row in range(height):
                out_ref[row, pl.ds(col + start, 8), :] = sums[row]

    start = 0
    for base_ref in base_refs:
        part(base_ref, start)
        start += base_ref.shape[1]

    @pl.loop(0, 2)
    def _(side):
        col = pl.multiple_of(side * (width - 8), 8)
        sums = [out_ref[row, pl.ds(col, 8), :] for row in range(height)]

        def load(row, tap):
            return strip[side, row - 3, pl.ds(tap + EDGE - 3, 8), :]

        tap_sums(sums, range(3, height + 3), load, spread_ref)
        for row in range(height):
            out_ref[row, pl.ds(col, 8), :] = sums[row]


def conv_kernel(start, flip, field_ref, kernel_ref, out_ref, padded, weights):
    spread(kernel_ref, weights, flip)
    pad_cols(field_ref, padded)
    local_taps(padded, weights, out_ref, start)


def mlp_kernel(
    first_ref,
    second_ref,
    field_ref,
    left_ref,
    right_ref,
    low_ref,
    high_ref,
    kernel_ref,
    cotangent_ref,
    mask_ref,
    gain_ref,
    w_in_ref,
    w_out_ref,
    g_ref,
    padded_ref,
    kept_ref,
    given_ref,
    gain_out_ref,
    side_ref,
    end_ref,
    conv,
    weights,
    strip,
    ends,
    pair_ref,
    gain_sum,
):
    height, width, channels = g_ref.shape
    transposed = (((1,), (1,)), ((), ()))
    spread(kernel_ref, weights, False)
    bases = (first_ref, second_ref)
    rest_taps(bases, left_ref, right_ref, low_ref, high_ref, weights, conv, strip, ends)
    padded_ref[3 : 3 + height, EDGE : EDGE + width, :] = field_ref[...]
    padded_ref[3 : 3 + height, :EDGE, :] = strip[0, :, :EDGE, :]
    padded_ref[3 : 3 + height, EDGE + width :, :] = strip[1, :, 2 * EDGE :, :]
    padded_ref[:3] = ends[0:3]
    padded_ref[3 + height :] = ends[3:6]
    pair_ref[...] = jnp.zeros(pair_ref.shape, f32)
    gain_sum[...] = jnp.zeros(gain_sum.shape, f32)
    gain = gain_ref[...]

    @pl.loop(0, height)
    def _(row):
        value = conv[row]
        center = value - jnp.mean(value, axis=-1, keepdims=True)
        scale = lax.rsqrt(jnp.mean(center * center, axis=-1, keepdims=True) + EPSILON)
        normed = center * scale
        ln_rows = (normed * gain).astype(bf16)
        mask = jnp.broadcast_to(mask_ref[pl.ds(row, 1), :].astype(f32), (channels, width)).T
        gy_rows = (mask * cotangent_ref[row].astype(f32)).astype(bf16)
        pre = jnp.dot(ln_rows, w_in_ref[...], preferred_element_type=f32)
        g_hidden = lax.dot_general(
            gy_rows, w_out_ref[...], transposed, preferred_element_type=f32
        )
        square = pre * pre
        half = 0.5 + 0.5 * jnp.tanh(pre * (ROOT + (ROOT * CUBIC) * square))
        hidden = pre * half
        slope = half + hidden * (1.0 - half) * (2 * ROOT + (6 * ROOT * CUBIC) * square)
        g_pre = (g_hidden * slope).astype(bf16)
        hidden = hidden.astype(bf16)
        pair_ref[0] += lax.dot_general(
            ln_rows, g_pre, (((0,), (0,)), ((), ())), preferred_element_type=f32
        )
        pair_ref[1] += lax.dot_general(
            gy_rows, hidden, (((0,), (0,)), ((), ())), preferred_element_type=f32
        )
        g_ln = lax.dot_general(g_pre, w_in_ref[...], transposed, preferred_element_type=f32)
        gain_sum[...] += jnp.sum((g_ln * normed).reshape(width // 8, 8, channels), axis=0)
        g_norm = g_ln * gain
        g_conv = (
            g_norm
            - jnp.mean(g_norm, axis=-1, keepdims=True)
            - normed * jnp.mean(g_norm * normed, axis=-1, keepdims=True)
        ) * scale
        g_ref[row] = g_conv
        side_ref[0, row] = g_conv[width - EDGE :].astype(bf16)
        side_ref[1, row] = g_conv[:EDGE].astype(bf16)

    end_ref[0] = g_ref[height - 3 :].astype(bf16)
    end_ref[1] = g_ref[:3].astype(bf16)
    gain_out_ref[...] = jnp.sum(gain_sum[...], axis=0, keepdims=True)
    odd = lax.rem(lax.axis_index("lat"), 2)
    kept_ref[...] = pair_ref[odd]
    given_ref[...] = pair_ref[1 - odd]


def taps_kernel(g_ref, field_ref, gain_ref, grad_ref):
    height, width, channels = g_ref.shape
    taps = field_ref.shape[0] - height + 1
    for col_tap in range(taps):

        def body(block, sums):
            sums = list(sums)
            col = pl.multiple_of(block * 8, 8)
            g_rows = [g_ref[row, pl.ds(col, 8), :] for row in range(height)]
            for row in range(height + taps - 1):
                value = field_ref[row, pl.ds(col + (col_tap + EDGE - 3), 8), :]
                for row_tap in range(taps):
                    if 0 <= row - row_tap < height:
                        sums[row_tap] = sums[row_tap] + g_rows[row - row_tap] * value
            return tuple(sums)

        start = tuple(jnp.zeros((8, channels), f32) for _ in range(taps))
        sums = lax.fori_loop(0, width // 8, body, start)
        for row_tap in range(taps):
            place = row_tap * taps + col_tap
            grad_ref[place : place + 1, :] = jnp.sum(sums[row_tap], axis=0, keepdims=True)
    grad_ref[taps * taps : taps * taps + 1, :] = gain_ref[...]


def state_kernel(
    base_ref,
    left_ref,
    right_ref,
    low_ref,
    high_ref,
    kernel_ref,
    cotangent_ref,
    state_ref,
    halves,
    weights,
    strip,
    ends,
    sums,
):
    height, width, channels = base_ref.shape
    spread(kernel_ref, weights, True)
    rest_taps((base_ref,), left_ref, right_ref, low_ref, high_ref, weights, sums, strip, ends)

    @pl.loop(0, height)
    def _(row):
        state = cotangent_ref[row].astype(f32) + sums[row]
        state_ref[row] = state
        high = state.astype(bf16)
        cells = pl.ds(pl.multiple_of(row * width, width), width)
        halves[cells, :channels] = high
        halves[cells, channels:] = (state - high.astype(f32)).astype(bf16)


def window_kernel(dense_ref, halves_ref, embed_ref, next_ref, window_ref, return_ref, late_ref):
    channels = window_ref.shape[1]
    own = embed_ref.shape[0]

    @pl.loop(0, window_ref.shape[0] // 256)
    def _(block):
        slots = pl.ds(pl.multiple_of(block * 256, 256), 256)
        both = jnp.dot(dense_ref[slots, :], halves_ref[...], preferred_element_type=f32)
        window_ref[slots, :] = both[:, :channels] + both[:, channels:]

    return_ref[...] = window_ref[own:].astype(bf16)
    rows = (((0,), (0,)), ((), ()))
    late_ref[...] = lax.dot_general(
        embed_ref[...], window_ref[:own].astype(bf16), rows, preferred_element_type=f32
    ) + lax.dot_general(next_ref[...], return_ref[...], rows, preferred_element_type=f32)


def finish_kernel(
    pair_ref, other_ref, late_ref, add_ref, in_ref, out_ref, projection_ref, kernel_ref, gain_ref
):
    even = lax.rem(lax.axis_index("lat"), 2) == 0

    @pl.when(even)
    def _():
        in_ref[...] = pair_ref[...]
        out_ref[...] = other_ref[...].T

    @pl.when(jnp.logical_not(even))
    def _():
        in_ref[...] = other_ref[...]
        out_ref[...] = pair_ref[...].T

    rows = projection_ref.shape[0]
    taps = kernel_ref.shape[0]
    late = late_ref[...].astype(f32) + add_ref[...].astype(f32)
    projection_ref[...] = late[:rows]
    for tap in range(taps):
        kernel_ref[tap] = late[rows + tap * taps : rows + (tap + 1) * taps]
    gain_ref[...] = late[rows + taps * taps :]


def shifted(x, axis, by, wrap=False):
    size = lax.axis_size(axis)
    pairs = [(i, (i + by) % size) for i in range(size) if wrap or 0 <= i + by < size]
    return lax.ppermute(x, axis, pairs)


def exchange(side, end):
    left = shifted(side[0], "lon", 1, True)
    right = shifted(side[1], "lon", -1, True)
    height = left.shape[0]
    to_high = jnp.concatenate([left[height - 3 :], end[0], right[height - 3 :]], axis=1)
    to_low = jnp.concatenate([left[:3], end[1], right[:3]], axis=1)
    low = shifted(to_high, "lat", 1)
    high = shifted(to_low, "lat", -1)
    return left, right, low, high


def xor_swap(x, axis, mask):
    size = lax.axis_size(axis)
    return lax.ppermute(x, axis, [(i, i ^ mask) for i in range(size)])


def steps_of(first=0):
    steps = []
    for axis in ("lat", "lon"):
        size = lax.axis_size(axis)
        if size & (size - 1):
            raise ValueError("axis size")
        steps += [(axis, 1 << k) for k in range(size.bit_length() - 1)]
    return steps[first:]


def fold(value, steps, name):
    for place, (axis, mask) in enumerate(steps):
        mine = value.astype(f32 if (axis, mask) == ("lat", 1) else bf16)
        other = xor_swap(mine, axis, mask)
        if name == "late" and place == len(steps) - 1:
            return mine, other
        value = mine.astype(f32) + other.astype(f32)
    return value


def step(
    ocean_state,
    cotangent,
    atm_embed,
    projection,
    dw_kernel,
    norm_gain,
    w_in,
    w_out,
    margin_index,
    margin_weight,
    sea_mask,
):
    cells_atm = atm_embed.shape[0]
    channels = projection.shape[1]
    height, width = ocean_state.shape[:2]
    taps = dw_kernel.shape[0]
    hidden = w_in.shape[1]
    slots = 2 * cells_atm
    cells = height * width
    grid = (height, width, channels)
    wide = width + 2 * EDGE
    tap_scratch = ((taps * taps, 8, channels), f32)
    strip = ((2, height, 3 * EDGE, channels), f32)
    ends = ((6, wide, channels), f32)
    own = lax.dot_general(
        projection, atm_embed, (((0,), (1,)), ((), ())), preferred_element_type=f32
    ).astype(bf16)
    following = shifted(own, "lat", -1)
    next_embed = shifted(atm_embed, "lat", -1)
    dense, part = kernel_call(
        margins_kernel,
        [((slots, cells), bf16), (grid, f32)],
        [],
        (margin_index.transpose(1, 0, 2), margin_weight.transpose(1, 0, 2), own),
        2 * cells * cells_atm * channels,
        8 << 20,
    )
    field, side, end = kernel_call(
        field_kernel,
        [(grid, f32), ((2, height, EDGE, channels), bf16), ((2, 3, width, channels), bf16)],
        [],
        (dense, following, part, ocean_state),
        2 * cells * cells_atm * channels,
        8 << 20,
    )
    left, right, low, high = exchange(side, end)
    half = (height, width // 2, channels)
    padded_scratch = ((height, wide, channels), f32)
    convs = [
        kernel_call(
            functools.partial(conv_kernel, start, False),
            [(half, f32)],
            [padded_scratch, tap_scratch],
            (field, dw_kernel),
            cells * channels * 49,
            8 << 20,
        )[0]
        for start in (0, width // 2)
    ]
    g_conv, padded, kept, given, gain_sum, side, end = kernel_call(
        mlp_kernel,
        [
            (grid, f32),
            ((height + 6, wide, channels), f32),
            ((channels, hidden), f32),
            ((channels, hidden), f32),
            ((1, channels), f32),
            ((2, height, EDGE, channels), bf16),
            ((2, 3, width, channels), bf16),
        ],
        [
            (grid, f32),
            tap_scratch,
            strip,
            ends,
            ((2, channels, hidden), f32),
            ((8, channels), f32),
        ],
        (
            *convs,
            field,
            left,
            right,
            low,
            high,
            dw_kernel,
            cotangent,
            sea_mask,
            norm_gain[None],
            w_in,
            w_out,
        ),
        cells * channels * hidden * 10,
        32 << 20,
    )
    left, right, low, high = exchange(side, end)
    received = xor_swap(given, "lat", 1)
    pair = fold(kept + received, steps_of(1), "early")
    other = xor_swap(pair, "lat", 1)
    (grad_taps,) = kernel_call(
        taps_kernel,
        [((taps * taps + 1, channels), f32)],
        [],
        (g_conv, padded, gain_sum),
        cells * channels * 98,
        16 << 20,
    )
    (back,) = kernel_call(
        functools.partial(conv_kernel, 0, True),
        [(grid, f32)],
        [padded_scratch, tap_scratch],
        (g_conv, dw_kernel),
        cells * channels * 98,
        16 << 20,
    )
    grad_state, halves = kernel_call(
        state_kernel,
        [(grid, f32), ((cells, 2 * channels), bf16)],
        [tap_scratch, strip, ends, (grid, f32)],
        (back, left, right, low, high, dw_kernel, cotangent),
        cells * channels * 20,
        8 << 20,
    )
    g_window, returned, grad_projection = kernel_call(
        window_kernel,
        [
            ((slots, channels), f32),
            ((cells_atm, channels), bf16),
            (projection.shape, f32),
        ],
        [],
        (dense, halves, atm_embed, next_embed),
        cells * slots * channels * 4,
        8 << 20,
    )
    returned = shifted(returned, "lat", 1)
    late = jnp.concatenate([grad_projection, grad_taps], axis=0)
    late, late_other = fold(late, steps_of(), "late")
    g_projected = (g_window[:cells_atm] + returned.astype(f32)).astype(bf16)
    grad_embed = lax.dot_general(
        g_projected, projection, (((1,), (1,)), ((), ())), preferred_element_type=f32
    )
    grad_in, grad_out, grad_projection, grad_kernel, grad_gain = kernel_call(
        finish_kernel,
        [
            (w_in.shape, f32),
            (w_out.shape, f32),
            (projection.shape, f32),
            (dw_kernel.shape, f32),
            ((1, channels), f32),
        ],
        [],
        (pair, other, late, late_other),
        channels * hidden,
        2 << 20,
    )
    return (
        grad_state,
        grad_embed,
        grad_projection,
        grad_kernel,
        grad_gain[0],
        grad_in,
        grad_out,
    )


def solution(mesh):
    return jax.shard_map(
        step,
        mesh=mesh,
        in_specs=(
            P("lat", "lon", None),
            P("lat", "lon", None),
            P(("lat", "lon"), None),
            P(),
            P(),
            P(),
            P(),
            P(),
            P(None, "lat", "lon"),
            P(None, "lat", "lon"),
            P("lat", "lon"),
        ),
        out_specs=(P("lat", "lon", None), P(("lat", "lon"), None), P(), P(), P(), P(), P()),
        check_vma=False,
    )
```
